32 devices in a mesh: req: 2 (over y), seq: 4 (over z), branch: 2 (over core), tp: 2 (over x).
Axes of the slice: x: 2, y: 2, z: 4, core: 2. Of those that a mesh axis runs over, the one named last changes fastest.
Arguments:
- projected: bfloat16 [2, 768, 3, 4096], P('branch', ('req', 'seq', 'tp')), parts along dimension 1, may hold values from -24 to 24
- hint_gain: float32 [4096], replicated, may hold values from 0.3 to 1.5
- block_map: int32 [4], replicated, may hold values from 0 to 3, each once
- token_perm: int32 [8, 48], replicated, may hold values from 0 to 47, each once within a row
Outputs:
- combined: bfloat16 [2, 768, 4096], P('branch', ('req', 'seq', 'tp')), parts along dimension 1
The draws below stay inside these ranges and needn't reach their ends.
There are 2 independent parts, one for each index of `req`. The reference program is written for one: setup_inputs(seed, part) draws one part's arguments, and reference() takes and returns one part's arrays. A program takes and returns all parts, laid end to end along the dimension named above; an argument that names none is the same for every part. Nothing has to cross between parts.
Inputs may be any that keep to these rules, and one draw needn't show every extreme that they name: `block_map`: a permutation of the 4 sequence shards. `token_perm`: each row is a permutation of 0 to 47.
All inputs are finite; a program needn't handle non-finite values.
Results may differ from the reference program's by a relative error of at most 0.0055.
Values may be sent and summed in bfloat16 or wider, within the bound.
A program may use at most 64 MiB of HBM per device.

```python
import math
import jax
import jax.numpy as jnp
from jax import lax

HD = 128
H = 32
TOK_DEV = 48
TOKENS = 384
ROW = 96
F = 4096
N_SEQ = 4
N_TP = 2


def draw_projected(key, part):
    streams = jax.random.split(jax.random.fold_in(key, 11), 10)
    grid_shape = (2, TOKENS, H, HD)
    drawn = jnp.clip(jax.random.normal(streams[0], (3,) + grid_shape, jnp.float32), -4.5, 4.5)
    row_scale = jnp.exp(jax.random.uniform(streams[1], (2, TOKENS, H, 1), jnp.float32, math.log(0.3), math.log(3.0)))
    head_scale = jnp.exp(jax.random.uniform(streams[2], (2, 1, H, 1), jnp.float32, math.log(0.25), math.log(2.5)))
    jitter = jnp.exp(jax.random.uniform(streams[9], (2, TOKENS, H, 1), jnp.float32, math.log(0.9), math.log(1.1)))
    col_scale = head_scale * jitter
    queries = drawn[0] * row_scale
    key_rows = drawn[1] * col_scale
    values = drawn[2]
    stacked = jnp.stack([queries, key_rows, values], axis=2)
    return jnp.clip(stacked, -24.0, 24.0).reshape(2, TOKENS, 3, H * HD).astype(jnp.bfloat16)


def setup_inputs(seed: int = 0, part: int = 0) -> dict:
    arg_keys = jax.random.split(jax.random.key(seed), 5)
    part_keys = jax.random.split(jax.random.fold_in(arg_keys[4], part), 5)
    return {
        "projected": draw_projected(jax.random.fold_in(jax.random.fold_in(arg_keys[4], part), 71), part),
        "hint_gain": jnp.clip(jnp.exp(jax.random.uniform(arg_keys[1], (F,), jnp.float32, math.log(0.3), math.log(1.5))), 0.3, 1.5),
        "block_map": jax.random.permutation(arg_keys[2], N_SEQ).astype(jnp.int32),
        "token_perm": jax.vmap(lambda own: jax.random.permutation(own, TOK_DEV))(jax.random.split(arg_keys[3], (N_SEQ * N_TP))).reshape((N_SEQ * N_TP, TOK_DEV)).astype(jnp.int32),
    }


def reference(projected, hint_gain, block_map, token_perm):
    scaling = 1.0 / math.sqrt(HD)

    def single_head(position):
        branch = position // H
        head_index = position % H
        zero = jnp.zeros((), jnp.int32)
        sliced = lax.dynamic_slice(projected, (branch, zero, zero, head_index * HD), (1, TOKENS, 3, HD))[0]
        queries = sliced[:, 0].astype(jnp.float32)
        key_rows = sliced[:, 1].astype(jnp.float32)
        values = sliced[:, 2].astype(jnp.float32)
        scores = jnp.dot(queries, key_rows.T, precision=lax.Precision.HIGHEST, preferred_element_type=jnp.float32) * scaling
        highest = lax.optimization_barrier(jnp.max(scores, axis=1, keepdims=True))
        weights = jnp.exp(scores - highest)
        totals = lax.optimization_barrier(jnp.sum(weights, axis=1, keepdims=True))
        rounded = weights.astype(jnp.bfloat16).astype(jnp.float32)
        attended = jnp.dot(rounded, values, precision=lax.Precision.HIGHEST, preferred_element_type=jnp.float32) / totals
        return attended.astype(jnp.bfloat16)
    heads = lax.map(single_head, jnp.arange(2 * H, dtype=jnp.int32))
    attended = heads.reshape(2, H, TOKENS, HD).transpose(0, 2, 1, 3).reshape(2, TOKENS, H * HD)
    attended = lax.optimization_barrier(attended)
    positions = jnp.arange(TOKENS, dtype=jnp.int32)
    source = ROW * block_map[positions // ROW] + TOK_DEV * (positions % ROW // TOK_DEV) + token_perm[positions // TOK_DEV, positions % TOK_DEV]
    control = attended[1][source].astype(jnp.float32)
    base_out = (attended[0].astype(jnp.float32) + hint_gain * control).astype(jnp.bfloat16)
    return jnp.stack([base_out, attended[1]])
```

```python
import functools
import math

import jax
import jax.numpy as jnp
from jax import lax
from jax.experimental import pallas as pl
from jax.experimental.pallas import tpu as pltpu
from jax.sharding import PartitionSpec as P

HD = 128
MESH = pl.DeviceIdType.MESH


key_block = 512


def passed_along(x, axis, by):
    count = lax.axis_size(axis)
    pairs = [(i, i + by) for i in range(count) if 0 <= i + by < count]
    return lax.ppermute(x, axis, pairs)


def attend(queries, key_rows, value_rows):
    row_count, columns = queries.shape
    local_heads = columns // HD
    query_heads = queries.reshape(row_count, local_heads, HD)
    scaling = 1.0 / math.sqrt(HD)
    initial = (
        jnp.full((local_heads, row_count), -jnp.inf, jnp.float32),
        jnp.zeros((local_heads, row_count), jnp.float32),
        jnp.zeros((local_heads, row_count, HD), jnp.float32),
    )
    running = initial
    key_piece = lax.all_gather(key_rows, "tp", axis=0, tiled=True)
    value_piece = lax.all_gather(value_rows, "tp", axis=0, tiled=True)
    length = key_piece.shape[0]
    step_rows = key_block if length % key_block == 0 else length
    number = length // step_rows
    key_blocks = key_piece.reshape(number, step_rows, local_heads, HD)
    value_blocks = value_piece.reshape(number, step_rows, local_heads, HD)

    def update(carried, blocks_now):
        highest, totals, summed = carried
        key_now, value_now = blocks_now
        scores = (
            jnp.einsum("qhd,khd->hqk", query_heads, key_now, preferred_element_type=jnp.float32)
            * scaling
        )
        new_highest = jnp.maximum(highest, jnp.max(scores, axis=2))
        fading = jnp.exp(highest - new_highest)
        weights = jnp.exp(scores - new_highest[..., None])
        totals = totals * fading + jnp.sum(weights, axis=2)
        summed = summed * fading[..., None] + jnp.einsum(
            "hqk,khd->hqd",
            weights.astype(jnp.bfloat16),
            value_now,
            preferred_element_type=jnp.float32,
        )
        return ((new_highest, totals, summed), None)

    running, unused = lax.scan(update, running, (key_blocks, value_blocks))
    highest, totals, summed = running
    result = summed / totals[..., None]
    return jnp.transpose(result, (1, 0, 2)).reshape(row_count, columns).astype(jnp.bfloat16)


def to_tokens(head_rows):
    return lax.all_to_all(head_rows, "seq", split_axis=0, concat_axis=1, tiled=True)


def on_device(projected, hint_gain, block_map, token_perm):
    block_rows = projected.shape[1]
    features = projected.shape[3]
    seq_count = lax.axis_size("seq")
    tp_count = lax.axis_size("tp")
    branch_index = lax.axis_index("branch")
    seq_index = lax.axis_index("seq")
    tp_index = lax.axis_index("tp")
    arrived = lax.all_to_all(projected[0], "seq", split_axis=2, concat_axis=0, tiled=True)
    columns = features // seq_count
    attended = attend(arrived[:, 0], arrived[:, 1], arrived[:, 2])
    attended = lax.optimization_barrier(attended)
    partner = passed_along(attended, "branch", -1)
    perm_table = token_perm.reshape(seq_count, tp_count, block_rows)
    column = lax.dynamic_index_in_dim(perm_table, tp_index, 1, keepdims=False)
    picked = (block_map[:, None] * block_rows + column).reshape(-1)
    control = jnp.take(partner, picked, axis=0).astype(jnp.float32)
    gain_slice = lax.dynamic_slice_in_dim(hint_gain, seq_index * columns, columns)
    summed = (attended.astype(jnp.float32) + gain_slice * control).astype(jnp.bfloat16)
    result = to_tokens(jnp.where(branch_index == 0, summed, attended))
    return result[None]


def attend_whole(queries, key_rows, value_rows):
    contract_last = (((1,), (1,)), ((), ()))
    scores = lax.dot_general(
        queries, key_rows, contract_last, preferred_element_type=jnp.float32
    ) * (1.0 / math.sqrt(HD))
    weights = jnp.exp(scores - jnp.max(scores, axis=1, keepdims=True))
    totals = jnp.sum(weights, axis=1, keepdims=True)
    summed = jnp.dot(
        weights.astype(jnp.bfloat16), value_rows, preferred_element_type=jnp.float32
    )
    return (summed / totals).astype(jnp.bfloat16)


def exchange_kernel(
    seq_count, tp_count, chunks,
    rows_ref, gain_ref, map_ref, perm_ref, out_ref,
    arrived, attended, hint, pick,
    in_send, in_recv, out_send, out_recv, hint_send, hint_recv,
):
    count = seq_count * tp_count
    block = rows_ref.shape[1]
    tokens = count * block
    branch = lax.axis_index("branch")
    me = lax.axis_index("seq") * tp_count + lax.axis_index("tp")

    def peer(k):
        return lax.rem(me + k, count)

    def coords(device):
        return {"seq": device // tp_count, "tp": lax.rem(device, tp_count)}

    def head_columns(device, chunk):
        return pl.ds(pl.multiple_of((device * chunks + chunk) * HD, HD), HD)

    def block_rows(device):
        return pl.ds(pl.multiple_of(device * block, block), block)

    barrier = pltpu.get_barrier_semaphore()
    for k in range(1, count):
        pl.semaphore_signal(barrier, inc=1, device_id=coords(peer(k)), device_id_type=MESH)
    pl.semaphore_signal(barrier, inc=1, device_id={"branch": 1 - branch}, device_id_type=MESH)
    pl.semaphore_wait(barrier, count)

    def in_copy(chunk, k):
        source = rows_ref.at[:, :, head_columns(peer(k), chunk)]
        target = arrived.at[chunk, :, block_rows(me), :]
        if k == 0:
            return pltpu.make_async_copy(source, target, in_recv.at[chunk, 0])
        return pltpu.make_async_remote_copy(
            src_ref=source, dst_ref=target,
            send_sem=in_send.at[chunk, k], recv_sem=in_recv.at[chunk, k],
            device_id=coords(peer(k)), device_id_type=MESH,
        )

    def out_copy(chunk, k):
        source = attended.at[chunk, block_rows(peer(k)), :]
        target = out_ref.at[:, head_columns(me, chunk)]
        if k == 0:
            return pltpu.make_async_copy(source, target, out_recv.at[chunk, 0])
        return pltpu.make_async_remote_copy(
            src_ref=source, dst_ref=target,
            send_sem=out_send.at[chunk, k], recv_sem=out_recv.at[chunk, k],
            device_id=coords(peer(k)), device_id_type=MESH,
        )

    def hint_copy(chunk):
        return pltpu.make_async_remote_copy(
            src_ref=attended.at[chunk], dst_ref=hint.at[chunk],
            send_sem=hint_send.at[chunk], recv_sem=hint_recv.at[chunk],
            device_id={"branch": 1 - branch}, device_id_type=MESH,
        )

    half = count // 2
    order = sorted(range(count), key=lambda k: abs(k - half))
    for chunk in range(chunks):
        for k in order:
            in_copy(chunk, k).start()

    @pl.when(branch == 0)
    def _():
        square = (block, block)
        diagonal = lax.broadcasted_iota(jnp.int32, square, 0) == lax.broadcasted_iota(jnp.int32, square, 1)
        lane = lax.broadcasted_iota(jnp.int32, (block, tokens), 1).astype(jnp.float32)
        for p in range(count):
            first = (map_ref[p // tp_count] * tp_count + p % tp_count) * block
            row = (perm_ref[p : p + 1, :] + first).astype(jnp.float32)
            column = jnp.sum(jnp.where(diagonal, row, 0.0), axis=1, keepdims=True)
            pick[p * block : (p + 1) * block, :] = jnp.where(lane == column, 1.0, 0.0).astype(jnp.bfloat16)

    for chunk in range(chunks):
        for k in order:
            if k == 0:
                in_copy(chunk, k).wait()
            else:
                in_copy(chunk, k).wait_recv()
        result = attend_whole(arrived[chunk, 0], arrived[chunk, 1], arrived[chunk, 2])

        @pl.when(branch == 1)
        def _():
            attended[chunk] = result
            hint_copy(chunk).start()

        @pl.when(branch == 0)
        def _():
            hint_copy(chunk).wait_recv()
            control = jnp.dot(pick[...], hint[chunk], preferred_element_type=jnp.float32)
            gain = gain_ref[pl.ds(me * chunks + chunk, 1), :]
            attended[chunk] = (result.astype(jnp.float32) + gain * control).astype(jnp.bfloat16)

        for k in order:
            out_copy(chunk, k).start()

    for chunk in range(chunks):
        @pl.when(branch == 1)
        def _():
            hint_copy(chunk).wait_send()

        for k in order:
            if k == 0:
                out_copy(chunk, k).wait()
            else:
                in_copy(chunk, k).wait_send()
                out_copy(chunk, k).wait()


def by_kernel(seq_count, tp_count, projected, hint_gain, block_map, token_perm):
    count = seq_count * tp_count
    block, features = projected.shape[1], projected.shape[3]
    chunks = features // HD // count
    tokens = count * block
    rows = jnp.transpose(projected[0], (1, 0, 2))
    dma = pltpu.SemaphoreType.DMA
    out = pl.pallas_call(
        functools.partial(exchange_kernel, seq_count, tp_count, chunks),
        out_shape=jax.ShapeDtypeStruct((block, features), projected.dtype),
        in_specs=[
            pl.BlockSpec(memory_space=pl.ANY),
            pl.BlockSpec(memory_space=pltpu.VMEM),
            pl.BlockSpec(memory_space=pltpu.SMEM),
            pl.BlockSpec(memory_space=pltpu.VMEM),
        ],
        out_specs=pl.BlockSpec(memory_space=pl.ANY),
        scratch_shapes=[
            pltpu.VMEM((chunks, 3, tokens, HD), projected.dtype),
            pltpu.VMEM((chunks, tokens, HD), projected.dtype),
            pltpu.VMEM((chunks, tokens, HD), projected.dtype),
            pltpu.VMEM((tokens, tokens), jnp.bfloat16),
            dma((chunks, count)), dma((chunks, count)),
            dma((chunks, count)), dma((chunks, count)),
            dma((chunks,)), dma((chunks,)),
        ],
        compiler_params=pltpu.CompilerParams(collective_id=0, has_side_effects=True),
    )(rows, hint_gain.reshape(features // HD, HD), block_map, token_perm)
    return out[None]


def solution(mesh):
    sizes = dict(mesh.shape)
    count = sizes["seq"] * sizes["tp"]

    def program(projected, hint_gain, block_map, token_perm):
        heads = projected.shape[3] // HD
        if heads % count == 0:
            return by_kernel(sizes["seq"], sizes["tp"], projected, hint_gain, block_map, token_perm)
        return on_device(projected, hint_gain, block_map, token_perm)

    return jax.shard_map(
        program,
        mesh=mesh,
        in_specs=(P("branch", ("req", "seq", "tp"), None, None), P(), P(), P()),
        out_specs=P("branch", ("req", "seq", "tp"), None),
        check_vma=False,
    )
```

```python
import functools
import math

import jax
import jax.numpy as jnp
from jax import lax
from jax.experimental import pallas as pl
from jax.experimental.pallas import tpu as pltpu
from jax.sharding import PartitionSpec as P

HD = 128
MESH = pl.DeviceIdType.MESH


key_block = 512


def passed_along(x, axis, by):
    count = lax.axis_size(axis)
    pairs = [(i, i + by) for i in range(count) if 0 <= i + by < count]
    return lax.ppermute(x, axis, pairs)


def attend(queries, key_rows, value_rows):
    row_count, columns = queries.shape
    local_heads = columns // HD
    query_heads = queries.reshape(row_count, local_heads, HD)
    scaling = 1.0 / math.sqrt(HD)
    initial = (
        jnp.full((local_heads, row_count), -jnp.inf, jnp.float32),
        jnp.zeros((local_heads, row_count), jnp.float32),
        jnp.zeros((local_heads, row_count, HD), jnp.float32),
    )
    running = initial
    key_piece = lax.all_gather(key_rows, "tp", axis=0, tiled=True)
    value_piece = lax.all_gather(value_rows, "tp", axis=0, tiled=True)
    length = key_piece.shape[0]
    step_rows = key_block if length % key_block == 0 else length
    number = length // step_rows
    key_blocks = key_piece.reshape(number, step_rows, local_heads, HD)
    value_blocks = value_piece.reshape(number, step_rows, local_heads, HD)

    def update(carried, blocks_now):
        highest, totals, summed = carried
        key_now, value_now = blocks_now
        scores = (
            jnp.einsum("qhd,khd->hqk", query_heads, key_now, preferred_element_type=jnp.float32)
            * scaling
        )
        new_highest = jnp.maximum(highest, jnp.max(scores, axis=2))
        fading = jnp.exp(highest - new_highest)
        weights = jnp.exp(scores - new_highest[..., None])
        totals = totals * fading + jnp.sum(weights, axis=2)
        summed = summed * fading[..., None] + jnp.einsum(
            "hqk,khd->hqd",
            weights.astype(jnp.bfloat16),
            value_now,
            preferred_element_type=jnp.float32,
        )
        return ((new_highest, totals, summed), None)

    running, unused = lax.scan(update, running, (key_blocks, value_blocks))
    highest, totals, summed = running
    result = summed / totals[..., None]
    return jnp.transpose(result, (1, 0, 2)).reshape(row_count, columns).astype(jnp.bfloat16)


def to_tokens(head_rows):
    return lax.all_to_all(head_rows, "seq", split_axis=0, concat_axis=1, tiled=True)


def on_device(projected, hint_gain, block_map, token_perm):
    block_rows = projected.shape[1]
    features = projected.shape[3]
    seq_count = lax.axis_size("seq")
    tp_count = lax.axis_size("tp")
    branch_index = lax.axis_index("branch")
    seq_index = lax.axis_index("seq")
    tp_index = lax.axis_index("tp")
    arrived = lax.all_to_all(projected[0], "seq", split_axis=2, concat_axis=0, tiled=True)
    columns = features // seq_count
    attended = attend(arrived[:, 0], arrived[:, 1], arrived[:, 2])
    attended = lax.optimization_barrier(attended)
    partner = passed_along(attended, "branch", -1)
    perm_table = token_perm.reshape(seq_count, tp_count, block_rows)
    column = lax.dynamic_index_in_dim(perm_table, tp_index, 1, keepdims=False)
    picked = (block_map[:, None] * block_rows + column).reshape(-1)
    control = jnp.take(partner, picked, axis=0).astype(jnp.float32)
    gain_slice = lax.dynamic_slice_in_dim(hint_gain, seq_index * columns, columns)
    summed = (attended.astype(jnp.float32) + gain_slice * control).astype(jnp.bfloat16)
    result = to_tokens(jnp.where(branch_index == 0, summed, attended))
    return result[None]


def attend_whole(queries, key_rows, value_rows):
    contract_last = (((1,), (1,)), ((), ()))
    scores = lax.dot_general(
        queries, key_rows, contract_last, preferred_element_type=jnp.float32
    ) * (1.0 / math.sqrt(HD))
    weights = jnp.exp(scores - jnp.max(scores, axis=1, keepdims=True))
    totals = jnp.sum(weights, axis=1, keepdims=True)
    summed = jnp.dot(
        weights.astype(jnp.bfloat16), value_rows, preferred_element_type=jnp.float32
    )
    return (summed / totals).astype(jnp.bfloat16)


def exchange_kernel(
    seq_count, tp_count, chunks,
    rows_ref, gain_in, map_in, perm_in, out_ref,
    arrived, attended, hint, pick, gain_ref, map_ref, perm_ref,
    in_send, in_recv, out_send, out_recv, hint_send, hint_recv, table_sem, from_above, from_below,
):
    count = seq_count * tp_count
    block = rows_ref.shape[1]
    tokens = count * block
    branch = lax.axis_index("branch")
    seq_index, tp_index = lax.axis_index("seq"), lax.axis_index("tp")
    me = seq_index * tp_count + tp_index
    half = seq_count // 2 if seq_count % 2 == 0 else seq_count
    side, place = seq_index // half, lax.rem(seq_index, half)
    sides = seq_count // half

    def peer(k):
        across, turn, shift = k // (half * tp_count), k // tp_count % half, k % tp_count
        there = lax.rem(side + across, sides) * half + lax.rem(place + turn, half)
        return there * tp_count + lax.rem(tp_index + shift, tp_count)

    def beside(shift):
        return lax.rem(tp_index + shift, tp_count)

    def coords(device):
        return {"seq": device // tp_count, "tp": lax.rem(device, tp_count)}

    def head_columns(device, chunk):
        return pl.ds(pl.multiple_of((device * chunks + chunk) * HD, HD), HD)

    def block_rows(device):
        return pl.ds(pl.multiple_of(device * block, block), block)

    def in_copy(chunk, device, origin):
        return pltpu.make_async_remote_copy(
            src_ref=rows_ref.at[:, :, head_columns(device, chunk)],
            dst_ref=arrived.at[chunk, :, block_rows(me), :],
            send_sem=in_send.at[chunk, device], recv_sem=in_recv.at[chunk, origin],
            device_id=coords(device), device_id_type=MESH,
        )

    def own_in_copy(chunk):
        return pltpu.make_async_copy(
            rows_ref.at[:, :, head_columns(me, chunk)],
            arrived.at[chunk, :, block_rows(me), :],
            in_recv.at[chunk, me],
        )

    def out_copy(chunk, k):
        source = attended.at[chunk, block_rows(peer(k)), :]
        target = out_ref.at[:, head_columns(me, chunk)]
        if k == 0:
            return pltpu.make_async_copy(source, target, out_recv.at[chunk, 0])
        return pltpu.make_async_remote_copy(
            src_ref=source, dst_ref=target,
            send_sem=out_send.at[chunk, k], recv_sem=out_recv.at[chunk, k],
            device_id=coords(peer(k)), device_id_type=MESH,
        )

    def hint_copy(chunk):
        return pltpu.make_async_remote_copy(
            src_ref=attended.at[chunk], dst_ref=hint.at[chunk],
            send_sem=hint_send.at[chunk], recv_sem=hint_recv.at[chunk],
            device_id={"branch": 1 - branch}, device_id_type=MESH,
        )

    order = range(count - 1, -1, -1)
    early = range(min(2, chunks))
    below, above = seq_index > 0, seq_index < seq_count - 1

    def send_row(row, shifts):
        for chunk in early:
            for shift in shifts:
                in_copy(chunk, row * tp_count + beside(shift), me).start()

    barrier = pltpu.get_barrier_semaphore()
    pl.semaphore_signal(barrier, inc=1, device_id={"branch": 1 - branch}, device_id_type=MESH)
    for shift in range(1, tp_count):
        pl.semaphore_signal(barrier, inc=1, device_id={"tp": beside(shift)}, device_id_type=MESH)

    @pl.when(below)
    def _():
        pl.semaphore_signal(barrier, inc=1, device_id={"seq": seq_index - 1}, device_id_type=MESH)

    @pl.when(above)
    def _():
        pl.semaphore_signal(barrier, inc=1, device_id={"seq": seq_index + 1}, device_id_type=MESH)

    reach = seq_count - 1
    beside_count = (seq_index + reach) // seq_count + (reach - seq_index + reach) // seq_count
    pl.semaphore_wait(barrier, tp_count + beside_count)

    for away in range(1, seq_count):
        @pl.when(below & (seq_index + away - 1 < seq_count))
        def _():
            pl.semaphore_signal(from_above.at[away], inc=1, device_id={"seq": seq_index - 1}, device_id_type=MESH)

        @pl.when(above & (seq_index - away + 1 >= 0))
        def _():
            pl.semaphore_signal(from_below.at[away], inc=1, device_id={"seq": seq_index + 1}, device_id_type=MESH)

        if away == 1:
            @pl.when(above)
            def _():
                send_row(seq_index + 1, [0])

            @pl.when(below)
            def _():
                send_row(seq_index - 1, [0])

            send_row(seq_index, range(1, tp_count))
            for chunk in range(chunks):
                own_in_copy(chunk).start()

        shifts = range(1 if away == 1 else 0, tp_count)

        @pl.when(seq_index + away < seq_count)
        def _():
            pl.semaphore_wait(from_above.at[away], 1)
            send_row(seq_index + away, shifts)

        @pl.when(seq_index - away >= 0)
        def _():
            pl.semaphore_wait(from_below.at[away], 1)
            send_row(seq_index - away, shifts)

    for chunk in range(len(early), chunks):
        for k in order:
            if k:
                in_copy(chunk, peer(k), me).start()

    @pl.when(branch == 0)
    def _():
        tables = [
            pltpu.make_async_copy(gain_in, gain_ref, table_sem.at[0]),
            pltpu.make_async_copy(map_in, map_ref, table_sem.at[1]),
            pltpu.make_async_copy(perm_in, perm_ref, table_sem.at[2]),
        ]
        for table in tables:
            table.start()
        for table in tables:
            table.wait()
        square = (block, block)
        diagonal = lax.broadcasted_iota(jnp.int32, square, 0) == lax.broadcasted_iota(jnp.int32, square, 1)
        lane = lax.broadcasted_iota(jnp.int32, (block, tokens), 1).astype(jnp.float32)
        for p in range(count):
            first = (map_ref[p // tp_count] * tp_count + p % tp_count) * block
            row = (perm_ref[p : p + 1, :] + first).astype(jnp.float32)
            column = jnp.sum(jnp.where(diagonal, row, 0.0), axis=1, keepdims=True)
            pick[p * block : (p + 1) * block, :] = jnp.where(lane == column, 1.0, 0.0).astype(jnp.bfloat16)

    for chunk in range(chunks):
        for k in order:
            if k == 0:
                own_in_copy(chunk).wait()
            else:
                in_copy(chunk, peer(k), peer(k)).wait_recv()
        result = attend_whole(arrived[chunk, 0], arrived[chunk, 1], arrived[chunk, 2])

        @pl.when(branch == 1)
        def _():
            attended[chunk] = result
            hint_copy(chunk).start()

        @pl.when(branch == 0)
        def _():
            hint_copy(chunk).wait_recv()
            control = jnp.dot(pick[...], hint[chunk], preferred_element_type=jnp.float32)
            gain = gain_ref[pl.ds(me * chunks + chunk, 1), :]
            attended[chunk] = (result.astype(jnp.float32) + gain * control).astype(jnp.bfloat16)

        for k in order:
            out_copy(chunk, k).start()

    for chunk in range(chunks):
        @pl.when(branch == 1)
        def _():
            hint_copy(chunk).wait_send()

        for k in order:
            if k == 0:
                out_copy(chunk, k).wait()
            else:
                in_copy(chunk, peer(k), me).wait_send()
                out_copy(chunk, k).wait()


def by_kernel(seq_count, tp_count, projected, hint_gain, block_map, token_perm):
    count = seq_count * tp_count
    block, features = projected.shape[1], projected.shape[3]
    chunks = features // HD // count
    tokens = count * block
    rows = jnp.transpose(projected[0], (1, 0, 2))
    dma = pltpu.SemaphoreType.DMA
    out = pl.pallas_call(
        functools.partial(exchange_kernel, seq_count, tp_count, chunks),
        out_shape=jax.ShapeDtypeStruct((block, features), projected.dtype),
        in_specs=[pl.BlockSpec(memory_space=pl.ANY)] * 4,
        out_specs=pl.BlockSpec(memory_space=pl.ANY),
        scratch_shapes=[
            pltpu.VMEM((chunks, 3, tokens, HD), projected.dtype),
            pltpu.VMEM((chunks, tokens, HD), projected.dtype),
            pltpu.VMEM((chunks, tokens, HD), projected.dtype),
            pltpu.VMEM((tokens, tokens), jnp.bfloat16),
            pltpu.VMEM((features // HD, HD), hint_gain.dtype),
            pltpu.SMEM(block_map.shape, block_map.dtype),
            pltpu.VMEM(token_perm.shape, token_perm.dtype),
            dma((chunks, count)), dma((chunks, count)),
            dma((chunks, count)), dma((chunks, count)),
            dma((chunks,)), dma((chunks,)), dma((3,)),
            pltpu.SemaphoreType.REGULAR((seq_count,)), pltpu.SemaphoreType.REGULAR((seq_count,)),
        ],
        compiler_params=pltpu.CompilerParams(collective_id=0, has_side_effects=True),
    )(rows, hint_gain.reshape(features // HD, HD), block_map, token_perm)
    return out[None]


def solution(mesh):
    sizes = dict(mesh.shape)
    count = sizes["seq"] * sizes["tp"]

    def program(projected, hint_gain, block_map, token_perm):
        heads = projected.shape[3] // HD
        if heads % count == 0:
            return by_kernel(sizes["seq"], sizes["tp"], projected, hint_gain, block_map, token_perm)
        return on_device(projected, hint_gain, block_map, token_perm)

    return jax.shard_map(
        program,
        mesh=mesh,
        in_specs=(P("branch", ("req", "seq", "tp"), None, None), P(), P(), P()),
        out_specs=P("branch", ("req", "seq", "tp"), None),
        check_vma=False,
    )
```

```python
import functools
import math

import jax
import jax.numpy as jnp
from jax import lax
from jax.experimental import pallas as pl
from jax.experimental.pallas import tpu as pltpu
from jax.sharding import PartitionSpec as P

HD = 128
MESH = pl.DeviceIdType.MESH


key_block = 512


def passed_along(x, axis, by):
    count = lax.axis_size(axis)
    pairs = [(i, i + by) for i in range(count) if 0 <= i + by < count]
    return lax.ppermute(x, axis, pairs)


def attend(queries, key_rows, value_rows):
    row_count, columns = queries.shape
    local_heads = columns // HD
    query_heads = queries.reshape(row_count, local_heads, HD)
    scaling = 1.0 / math.sqrt(HD)
    initial = (
        jnp.full((local_heads, row_count), -jnp.inf, jnp.float32),
        jnp.zeros((local_heads, row_count), jnp.float32),
        jnp.zeros((local_heads, row_count, HD), jnp.float32),
    )
    running = initial
    key_piece = lax.all_gather(key_rows, "tp", axis=0, tiled=True)
    value_piece = lax.all_gather(value_rows, "tp", axis=0, tiled=True)
    length = key_piece.shape[0]
    step_rows = key_block if length % key_block == 0 else length
    number = length // step_rows
    key_blocks = key_piece.reshape(number, step_rows, local_heads, HD)
    value_blocks = value_piece.reshape(number, step_rows, local_heads, HD)

    def update(carried, blocks_now):
        highest, totals, summed = carried
        key_now, value_now = blocks_now
        scores = (
            jnp.einsum("qhd,khd->hqk", query_heads, key_now, preferred_element_type=jnp.float32)
            * scaling
        )
        new_highest = jnp.maximum(highest, jnp.max(scores, axis=2))
        fading = jnp.exp(highest - new_highest)
        weights = jnp.exp(scores - new_highest[..., None])
        totals = totals * fading + jnp.sum(weights, axis=2)
        summed = summed * fading[..., None] + jnp.einsum(
            "hqk,khd->hqd",
            weights.astype(jnp.bfloat16),
            value_now,
            preferred_element_type=jnp.float32,
        )
        return ((new_highest, totals, summed), None)

    running, unused = lax.scan(update, running, (key_blocks, value_blocks))
    highest, totals, summed = running
    result = summed / totals[..., None]
    return jnp.transpose(result, (1, 0, 2)).reshape(row_count, columns).astype(jnp.bfloat16)


def to_tokens(head_rows):
    return lax.all_to_all(head_rows, "seq", split_axis=0, concat_axis=1, tiled=True)


def on_device(projected, hint_gain, block_map, token_perm):
    block_rows = projected.shape[1]
    features = projected.shape[3]
    seq_count = lax.axis_size("seq")
    tp_count = lax.axis_size("tp")
    branch_index = lax.axis_index("branch")
    seq_index = lax.axis_index("seq")
    tp_index = lax.axis_index("tp")
    arrived = lax.all_to_all(projected[0], "seq", split_axis=2, concat_axis=0, tiled=True)
    columns = features // seq_count
    attended = attend(arrived[:, 0], arrived[:, 1], arrived[:, 2])
    attended = lax.optimization_barrier(attended)
    partner = passed_along(attended, "branch", -1)
    perm_table = token_perm.reshape(seq_count, tp_count, block_rows)
    column = lax.dynamic_index_in_dim(perm_table, tp_index, 1, keepdims=False)
    picked = (block_map[:, None] * block_rows + column).reshape(-1)
    control = jnp.take(partner, picked, axis=0).astype(jnp.float32)
    gain_slice = lax.dynamic_slice_in_dim(hint_gain, seq_index * columns, columns)
    summed = (attended.astype(jnp.float32) + gain_slice * control).astype(jnp.bfloat16)
    result = to_tokens(jnp.where(branch_index == 0, summed, attended))
    return result[None]


def attend_whole(queries, key_rows, value_rows):
    contract_last = (((1,), (1,)), ((), ()))
    scores = lax.dot_general(
        queries, key_rows, contract_last, preferred_element_type=jnp.float32
    ) * (1.0 / math.sqrt(HD))
    weights = jnp.exp(scores - jnp.max(scores, axis=1, keepdims=True))
    totals = jnp.sum(weights, axis=1, keepdims=True)
    summed = jnp.dot(
        weights.astype(jnp.bfloat16), value_rows, preferred_element_type=jnp.float32
    )
    return (summed / totals).astype(jnp.bfloat16)


def exchange_kernel(
    seq_count, tp_count, chunks,
    rows_ref, gain_in, map_in, perm_in, out_ref,
    arrived, attended, hint, pick, gain_ref, map_ref, perm_ref,
    in_send, in_recv, out_send, out_recv, hint_send, hint_recv, table_sem, from_above, from_below,
):
    count = seq_count * tp_count
    block = rows_ref.shape[1]
    tokens = count * block
    branch = lax.axis_index("branch")
    seq_index, tp_index = lax.axis_index("seq"), lax.axis_index("tp")
    me = seq_index * tp_count + tp_index
    half = seq_count // 2 if seq_count % 2 == 0 else seq_count
    side, place = seq_index // half, lax.rem(seq_index, half)
    sides = seq_count // half

    def peer(k):
        across, turn, shift = k // (half * tp_count), k // tp_count % half, k % tp_count
        there = lax.rem(side + across, sides) * half + lax.rem(place + turn, half)
        return there * tp_count + lax.rem(tp_index + shift, tp_count)

    def beside(shift):
        return lax.rem(tp_index + shift, tp_count)

    def coords(device):
        return {"seq": device // tp_count, "tp": lax.rem(device, tp_count)}

    def head_columns(device, chunk):
        return pl.ds(pl.multiple_of((device * chunks + chunk) * HD, HD), HD)

    def block_rows(device):
        return pl.ds(pl.multiple_of(device * block, block), block)

    def in_copy(chunk, device, origin):
        return pltpu.make_async_remote_copy(
            src_ref=rows_ref.at[:, :, head_columns(device, chunk)],
            dst_ref=arrived.at[chunk, :, block_rows(me), :],
            send_sem=in_send.at[chunk, device], recv_sem=in_recv.at[chunk, origin],
            device_id=coords(device), device_id_type=MESH,
        )

    def own_in_copy(chunk):
        return pltpu.make_async_copy(
            rows_ref.at[:, :, head_columns(me, chunk)],
            arrived.at[chunk, :, block_rows(me), :],
            in_recv.at[chunk, me],
        )

    def out_copy(chunk, k):
        source = attended.at[chunk, block_rows(peer(k)), :]
        target = out_ref.at[:, head_columns(me, chunk)]
        if k == 0:
            return pltpu.make_async_copy(source, target, out_recv.at[chunk, 0])
        return pltpu.make_async_remote_copy(
            src_ref=source, dst_ref=target,
            send_sem=out_send.at[chunk, k], recv_sem=out_recv.at[chunk, k],
            device_id=coords(peer(k)), device_id_type=MESH,
        )

    def hint_copy(chunk):
        return pltpu.make_async_remote_copy(
            src_ref=attended.at[chunk], dst_ref=hint.at[chunk],
            send_sem=hint_send.at[chunk], recv_sem=hint_recv.at[chunk],
            device_id={"branch": 1 - branch}, device_id_type=MESH,
        )

    order = range(count - 1, -1, -1)
    early = range(min(3, chunks))
    below, above = seq_index > 0, seq_index < seq_count - 1

    def send_row(row, shifts):
        for chunk in early:
            for shift in shifts:
                in_copy(chunk, row * tp_count + beside(shift), me).start()

    barrier = pltpu.get_barrier_semaphore()
    pl.semaphore_signal(barrier, inc=1, device_id={"branch": 1 - branch}, device_id_type=MESH)
    for shift in range(1, tp_count):
        pl.semaphore_signal(barrier, inc=1, device_id={"tp": beside(shift)}, device_id_type=MESH)

    @pl.when(below)
    def _():
        pl.semaphore_signal(barrier, inc=1, device_id={"seq": seq_index - 1}, device_id_type=MESH)

    @pl.when(above)
    def _():
        pl.semaphore_signal(barrier, inc=1, device_id={"seq": seq_index + 1}, device_id_type=MESH)

    reach = seq_count - 1
    beside_count = (seq_index + reach) // seq_count + (reach - seq_index + reach) // seq_count
    pl.semaphore_wait(barrier, tp_count + beside_count)

    for away in range(1, seq_count):
        @pl.when(below & (seq_index + away - 1 < seq_count))
        def _():
            pl.semaphore_signal(from_above.at[away], inc=1, device_id={"seq": seq_index - 1}, device_id_type=MESH)

        @pl.when(above & (seq_index - away + 1 >= 0))
        def _():
            pl.semaphore_signal(from_below.at[away], inc=1, device_id={"seq": seq_index + 1}, device_id_type=MESH)

        if away == 1:
            @pl.when(above)
            def _():
                send_row(seq_index + 1, [0])

            @pl.when(below)
            def _():
                send_row(seq_index - 1, [0])

            send_row(seq_index, range(1, tp_count))
            for chunk in range(chunks):
                own_in_copy(chunk).start()

        shifts = range(1 if away == 1 else 0, tp_count)

        @pl.when(seq_index + away < seq_count)
        def _():
            pl.semaphore_wait(from_above.at[away], 1)
            send_row(seq_index + away, shifts)

        @pl.when(seq_index - away >= 0)
        def _():
            pl.semaphore_wait(from_below.at[away], 1)
            send_row(seq_index - away, shifts)

    for chunk in range(len(early), chunks):
        for k in order:
            if k:
                in_copy(chunk, peer(k), me).start()

    @pl.when(branch == 0)
    def _():
        tables = [
            pltpu.make_async_copy(gain_in, gain_ref, table_sem.at[0]),
            pltpu.make_async_copy(map_in, map_ref, table_sem.at[1]),
            pltpu.make_async_copy(perm_in, perm_ref, table_sem.at[2]),
        ]
        for table in tables:
            table.start()
        for table in tables:
            table.wait()
        square = (block, block)
        diagonal = lax.broadcasted_iota(jnp.int32, square, 0) == lax.broadcasted_iota(jnp.int32, square, 1)
        lane = lax.broadcasted_iota(jnp.int32, (block, tokens), 1).astype(jnp.float32)
        for p in range(count):
            first = (map_ref[p // tp_count] * tp_count + p % tp_count) * block
            row = (perm_ref[p : p + 1, :] + first).astype(jnp.float32)
            column = jnp.sum(jnp.where(diagonal, row, 0.0), axis=1, keepdims=True)
            pick[p * block : (p + 1) * block, :] = jnp.where(lane == column, 1.0, 0.0).astype(jnp.bfloat16)

    for chunk in range(chunks):
        for k in order:
            if k == 0:
                own_in_copy(chunk).wait()
            else:
                in_copy(chunk, peer(k), peer(k)).wait_recv()
        result = attend_whole(arrived[chunk, 0], arrived[chunk, 1], arrived[chunk, 2])

        @pl.when(branch == 1)
        def _():
            attended[chunk] = result
            hint_copy(chunk).start()

        @pl.when(branch == 0)
        def _():
            hint_copy(chunk).wait_recv()
            control = jnp.dot(pick[...], hint[chunk], preferred_element_type=jnp.float32)
            gain = gain_ref[pl.ds(me * chunks + chunk, 1), :]
            attended[chunk] = (result.astype(jnp.float32) + gain * control).astype(jnp.bfloat16)

        for k in order:
            out_copy(chunk, k).start()

    for chunk in range(chunks):
        @pl.when(branch == 1)
        def _():
            hint_copy(chunk).wait_send()

        for k in order:
            if k == 0:
                out_copy(chunk, k).wait()
            else:
                in_copy(chunk, peer(k), me).wait_send()
                out_copy(chunk, k).wait()


def by_kernel(seq_count, tp_count, projected, hint_gain, block_map, token_perm):
    count = seq_count * tp_count
    block, features = projected.shape[1], projected.shape[3]
    chunks = features // HD // count
    tokens = count * block
    rows = jnp.transpose(projected[0], (1, 0, 2))
    dma = pltpu.SemaphoreType.DMA
    out = pl.pallas_call(
        functools.partial(exchange_kernel, seq_count, tp_count, chunks),
        out_shape=pltpu.VMEM((block, features), projected.dtype),
        in_specs=[pl.BlockSpec(memory_space=pl.ANY)] * 4,
        out_specs=pl.BlockSpec(memory_space=pl.ANY),
        scratch_shapes=[
            pltpu.VMEM((chunks, 3, tokens, HD), projected.dtype),
            pltpu.VMEM((chunks, tokens, HD), projected.dtype),
            pltpu.VMEM((chunks, tokens, HD), projected.dtype),
            pltpu.VMEM((tokens, tokens), jnp.bfloat16),
            pltpu.VMEM((features // HD, HD), hint_gain.dtype),
            pltpu.SMEM(block_map.shape, block_map.dtype),
            pltpu.VMEM(token_perm.shape, token_perm.dtype),
            dma((chunks, count)), dma((chunks, count)),
            dma((chunks, count)), dma((chunks, count)),
            dma((chunks,)), dma((chunks,)), dma((3,)),
            pltpu.SemaphoreType.REGULAR((seq_count,)), pltpu.SemaphoreType.REGULAR((seq_count,)),
        ],
        compiler_params=pltpu.CompilerParams(collective_id=0, has_side_effects=True),
    )(rows, hint_gain.reshape(features // HD, HD), block_map, token_perm)
    return out[None]


def solution(mesh):
    sizes = dict(mesh.shape)
    count = sizes["seq"] * sizes["tp"]

    def program(projected, hint_gain, block_map, token_perm):
        heads = projected.shape[3] // HD
        if heads % count == 0:
            return by_kernel(sizes["seq"], sizes["tp"], projected, hint_gain, block_map, token_perm)
        return on_device(projected, hint_gain, block_map, token_perm)

    return jax.shard_map(
        program,
        mesh=mesh,
        in_specs=(P("branch", ("req", "seq", "tp"), None, None), P(), P(), P()),
        out_specs=P("branch", ("req", "seq", "tp"), None),
        check_vma=False,
    )
```
